32 devices in a mesh: rows: 16 (over z, y, core), cols: 2 (over x).
Axes of the slice: x: 2, y: 2, z: 4, core: 2. Of those that a mesh axis runs over, the one named last changes fastest.
Arguments:
- features: bfloat16 [4096, 128], P('rows', 'cols'), may hold values from -6 to 6
- adj_tiles: bfloat16 [1536, 128, 128], P('rows'), may hold values from -0.109375 to 0.109375
- tile_src: int32 [1536], P('rows'), may hold values from 0 to 31, as said below
- tile_dst: int32 [1536], P('rows'), may hold values from 0 to 1, as said below
- tile_count: int32 [16], P('rows'), may hold values from 24 to 96, as said below
- cluster_size: int32 [32], P('rows'), may hold values from 64 to 128, as said below
- weight: bfloat16 [128, 256], P(None, 'cols'), may hold values from -0.5 to 0.5
- bias: float32 [256], P('cols'), may hold values from -3 to 3
- grad_out: bfloat16 [4096, 256], P('rows', 'cols'), may hold values from -6 to 6
Outputs:
- hidden: bfloat16 [4096, 256], P('rows', 'cols')
- grad_weight: float32 [128, 256], P(None, 'cols')
- grad_bias: float32 [256], P('cols')
- grad_features: bfloat16 [4096, 128], P('rows', 'cols')
The draws below stay inside these ranges and needn't reach their ends.
Inputs may be any that keep to these rules, and one draw needn't show every extreme that they name: In row group r, slots 0 to tile_count[r] - 1 of its 96 slots hold tiles, in non-decreasing order of tile_src; the later slots are unused: their tile_src and tile_dst hold 0, and their adj_tiles hold arbitrary values that must not contribute. A used slot's column cluster belongs to row group r itself or to a row group whose index differs from r in exactly one bit (row group g holds clusters g * 2 to g * 2 + 1). Equal (row, column) pairs may repeat and then add. `tile_dst`: unused slots hold 0. `tile_count`: some row groups use all 96 slots. `cluster_size`: the real nodes of a cluster are its first ones; some cluster is full.
All inputs are finite; a program needn't handle non-finite values.
Results may differ from the reference program's by a relative error of at most 0.006.
Values may be sent and summed in bfloat16 or wider, within the bound.
No kernel may reach another device: no remote copies, remote signals or barrier semaphores. Data moves between devices by JAX's collectives and lax.ppermute only.
A program may use at most 64 MiB of HBM per device.

```python
import math
import jax
import jax.numpy as jnp
from jax import lax

F = 128
HID = 256
CLS = 128
TPC = 48
CL_DEV = 2
TILES_DEV = 96
CLUSTERS = 32
NODES = 4096
ROW_SLOTS = 1536
LEVELS = 4


def tile_layout(key):
    group_count = ROW_SLOTS // TILES_DEV
    key_rank, key_light, key_level, key_within, key_dst = jax.random.split(jax.random.fold_in(key, 11), 5)
    row_rank = jax.random.permutation(key_rank, group_count)
    light_count = jax.random.randint(key_light, (group_count,), TILES_DEV // 4, TILES_DEV // 2 + 1)
    live_count = jnp.where(row_rank < max(group_count // 8, 1), TILES_DEV, light_count).astype(jnp.int32)
    slot_ids = jnp.arange(TILES_DEV, dtype=jnp.int32)
    in_use = slot_ids[None, :] < live_count[:, None]
    group_ids = jnp.arange(group_count, dtype=jnp.int32)[:, None]
    level = jax.random.randint(key_level, (group_count, TILES_DEV), 0, LEVELS + 1).astype(jnp.int32)
    flipped = jnp.bitwise_xor(group_ids, jnp.left_shift(jnp.ones_like(level), jnp.minimum(level, LEVELS - 1)))
    neighbour = jnp.where(level == LEVELS, group_ids, flipped)
    within = jax.random.randint(key_within, (group_count, TILES_DEV), 0, CL_DEV).astype(jnp.int32)
    drawn_src = neighbour * CL_DEV + within
    drawn_src = drawn_src.at[0, 0].set(0)
    drawn_src = drawn_src.at[group_count - 1, 0].set(CLUSTERS - 1)
    ordered = jnp.sort(jnp.where(in_use, drawn_src, CLUSTERS), axis=1)
    sources = jnp.where(in_use, ordered, 0).reshape(-1).astype(jnp.int32)
    drawn_dst = jax.random.randint(key_dst, (group_count, TILES_DEV), 0, CL_DEV)
    targets = jnp.where(in_use, drawn_dst, 0).reshape(-1).astype(jnp.int32)
    return (sources, targets, live_count)


def draw_tile_src(key, part):
    return tile_layout(key)[0]


def draw_tile_dst(key, part):
    return tile_layout(key)[1]


def draw_tile_count(key, part):
    return tile_layout(key)[2]


def draw_cluster_size(key, part):
    key_size, key_full = jax.random.split(jax.random.fold_in(key, 23))
    sizes = jax.random.randint(key_size, (CLUSTERS,), CLS // 2, CLS + 1)
    full_at = jax.random.randint(key_full, (), 0, CLUSTERS)
    return jnp.where(jnp.arange(CLUSTERS) == full_at, CLS, sizes).astype(jnp.int32)


def steps_of(key, extent, cuts, low, top_value):
    loudness = 1.0
    for dim, blocks in cuts:
        steps = jax.random.uniform(jax.random.fold_in(jax.random.fold_in(key, 6), dim), (blocks,), jnp.float32, low / len(cuts), top_value / len(cuts))
        loudness = loudness * jnp.repeat(jnp.exp(steps), extent[dim] // blocks).reshape((-1,) + (1,) * (len(extent) - 1 - dim))
    return loudness


def normal_values(stream_key, extent, spread, limit, cuts=(), kind=jnp.bfloat16):
    factor_of = steps_of(stream_key, extent, cuts, -0.22, 0.18) if cuts else 1.0
    drawn = jax.random.normal(stream_key, extent, jnp.float32) * spread * factor_of
    return jnp.minimum(jnp.maximum(drawn, -limit), limit).astype(kind)


def setup_inputs(seed: int = 0) -> dict:
    splits = jax.random.split(jax.random.key(seed), 10)
    features = normal_values(splits[0], (NODES, F), 1.0, 6.0, ((0, 16), (1, 2)))
    adj_tiles = normal_values(splits[1], (ROW_SLOTS, CLS, CLS), (CLS * TPC // 2) ** -0.5, 0.109375, ((0, 16),))
    tile_src = draw_tile_src(jax.random.fold_in(splits[9], 71), 0)
    tile_dst = draw_tile_dst(jax.random.fold_in(splits[9], 71), 0)
    tile_count = draw_tile_count(jax.random.fold_in(splits[9], 71), 0)
    cluster_size = draw_cluster_size(jax.random.fold_in(splits[9], 71), 0)
    weight = normal_values(splits[6], (F, HID), F ** -0.5, 0.5, ((1, 2),))
    bias = normal_values(splits[7], (HID,), 0.5, 3.0, ((0, 2),), jnp.float32)
    grad_out = normal_values(splits[8], (NODES, HID), 1.0, 6.0, ((0, 16), (1, 2)))
    return dict(features=features, adj_tiles=adj_tiles, tile_src=tile_src, tile_dst=tile_dst, tile_count=tile_count, cluster_size=cluster_size, weight=weight, bias=bias, grad_out=grad_out)


def reference(features, adj_tiles, tile_src, tile_dst, tile_count, cluster_size, weight, bias, grad_out):
    row_groups = CLUSTERS // CL_DEV
    node_ids = jnp.arange(CLS, dtype=jnp.int32)
    live_node = (node_ids[None, :] < cluster_size[:, None]).astype(jnp.float32).reshape(NODES, 1)
    masked = (features.astype(jnp.float32) * live_node).astype(jnp.bfloat16)
    blocks = masked.reshape(CLUSTERS, CLS, F)
    tile_data = adj_tiles.reshape(row_groups, TILES_DEV, CLS, CLS)
    sources = tile_src.reshape(row_groups, TILES_DEV)
    targets = tile_dst.reshape(row_groups, TILES_DEV)
    slot_ids = jnp.arange(TILES_DEV, dtype=jnp.int32)

    def forward_row(packed):
        group_tiles, group_src, group_dst, group_count = packed
        in_use = (slot_ids < group_count).astype(jnp.float32)
        taken_rows = blocks[group_src].astype(jnp.float32)
        products = jnp.einsum('tij,tjf->tif', group_tiles.astype(jnp.float32), taken_rows) * in_use[:, None, None]
        return jnp.zeros((CL_DEV, CLS, F), jnp.float32).at[group_dst].add(products)
    agg = lax.map(forward_row, (tile_data, sources, targets, tile_count)).reshape(NODES, F).astype(jnp.bfloat16)
    pre_activation = jnp.dot(agg, weight, preferred_element_type=jnp.float32) + bias
    sigmoid_pre = jax.nn.sigmoid(pre_activation)
    hidden = (pre_activation * sigmoid_pre * live_node).astype(jnp.bfloat16)
    grad_pre = (grad_out.astype(jnp.float32) * sigmoid_pre * (1.0 + pre_activation * (1.0 - sigmoid_pre)) * live_node).astype(jnp.bfloat16)
    grad_scale = 1.0 / math.sqrt(NODES)
    grad_weight = jnp.dot(agg.T, grad_pre, preferred_element_type=jnp.float32) * grad_scale
    grad_bias = lax.optimization_barrier(jnp.sum(grad_pre.astype(jnp.float32), axis=0)) * grad_scale
    grad_agg = jnp.dot(grad_pre, weight.T, preferred_element_type=jnp.float32).astype(jnp.bfloat16).reshape(CLUSTERS, CLS, F)

    def backward_row(totals, packed):
        group_tiles, group_src, group_dst, group_count, group_index = packed
        in_use = (slot_ids < group_count).astype(jnp.float32)
        taken_rows = grad_agg[group_index * CL_DEV + group_dst].astype(jnp.float32)
        products = jnp.einsum('tji,tjf->tif', group_tiles.astype(jnp.float32), taken_rows) * in_use[:, None, None]
        return (totals.at[group_src].add(products), None)
    group_ids = jnp.arange(row_groups, dtype=jnp.int32)
    totals, unused = lax.scan(backward_row, jnp.zeros((CLUSTERS, CLS, F), jnp.float32), (tile_data, sources, targets, tile_count, group_ids))
    grad_features = (totals.reshape(NODES, F) * live_node).astype(jnp.bfloat16)
    return (hidden, grad_weight, grad_bias, grad_features)
```

```python
import functools
import math

import jax
import jax.numpy as jnp
from jax import lax
from jax.experimental import pallas as pl
from jax.experimental.pallas import tpu as pltpu
from jax.sharding import PartitionSpec as P


TILE_GROUP = 16
F32, BF16 = jnp.float32, jnp.bfloat16
VMEM = pl.BlockSpec(memory_space=pltpu.VMEM)
SMEM = pl.BlockSpec(memory_space=pltpu.SMEM)
HBM = pl.BlockSpec(memory_space=pl.ANY)


def partner(shard, axis, bit):
    return lax.ppermute(shard, axis, [(i, i ^ 1 << bit) for i in range(lax.axis_size(axis))])


def dot(a, b, contract=(1, 0)):
    return lax.dot_general(
        a, b, (((contract[0],), (contract[1],)), ((), ())), preferred_element_type=F32
    )


def live_rows(sizes, clusters, width):
    node = lax.broadcasted_iota(jnp.int32, (width, 1), 0)
    return jnp.concatenate([(node < sizes[c]).astype(F32) for c in range(clusters)], axis=0)


def build_kernel(levels, clusters, tiles, src, dst, count, gout, weight, bias, hi, lo, pack, acc, held, sems, side):
    slots, width = tiles.shape[0], tiles.shape[1]
    rows, hidden = gout.shape
    feats = weight.shape[0]
    used = count[0]
    me = lax.axis_index("rows")
    starts = list(range(0, slots, TILE_GROUP))

    def fetch(first):
        size = min(TILE_GROUP, slots - first)
        return pltpu.make_async_copy(
            tiles.at[pl.ds(first, size)], held.at[pl.ds(first, size)], sems.at[first // TILE_GROUP]
        )

    for first in starts:
        @pl.when(first < used)
        def _(first=first):
            fetch(first).start()
    sides = (
        pltpu.make_async_copy(gout, pack.at[pl.ds(0, rows)], side.at[0]),
        pltpu.make_async_copy(weight, pack.at[pl.ds(rows, feats)], side.at[1]),
    )
    for copy in sides:
        copy.start()
    value = bias[...]
    top = value.astype(BF16).astype(F32)
    rest = value - top
    middle = rest.astype(BF16).astype(F32)
    row = lax.broadcasted_iota(jnp.int32, (16, hidden), 0)
    parts = jnp.where(row == 0, top, jnp.where(row == 1, middle, jnp.where(row == 2, rest - middle, 0.0)))
    pack[pl.ds(rows + feats, 16), :] = parts.astype(BF16)
    acc[...] = jnp.zeros_like(acc)

    def add(slot, carry):
        source = src[slot]
        group = lax.div(source, clusters)
        differs = jnp.bitwise_xor(group, me)
        column = source - group * clusters
        for bit in range(levels):
            column = column + jnp.where(differs == 1 << bit, (bit + 1) * clusters, 0)
        at = (
            pl.ds(pl.multiple_of(dst[slot] * width, width), width),
            pl.ds(pl.multiple_of(column * width, width), width),
        )
        acc[at] = acc[at] + held[slot].astype(F32)
        return carry

    for first in starts:
        @pl.when(first < used)
        def _(first=first):
            fetch(first).wait()
            lax.fori_loop(first, jnp.minimum(first + TILE_GROUP, used), add, 0)

    total = acc[...]
    high = total.astype(BF16)
    hi[...] = high
    lo[...] = (total - high.astype(F32)).astype(BF16)
    for copy in sides:
        copy.wait()


def merge_kernel(clusters, own, other, sizes, out):
    mine, theirs = own[...].astype(F32), other[...].astype(F32)
    first = lax.axis_index("cols") == 0
    both = jnp.concatenate(
        [jnp.where(first, mine, theirs), jnp.where(first, theirs, mine)], axis=0
    )
    live = live_rows(sizes, clusters, own.shape[1] // clusters)
    out[...] = (both.T * live).astype(BF16)


def main_kernel(levels, clusters, *refs):
    hi, lo, gout, weight, bias, pack, sizes = refs[:7]
    tables = refs[7 : 8 + levels]
    hidden_out, sums, grad_out_t = refs[8 + levels :]
    nodes, feats = tables[0].shape
    half = grad_out_t.shape[0]
    agg = jnp.zeros((nodes, feats), F32)
    for level, table in enumerate(tables):
        value = table[...]
        at = (slice(None), pl.ds(level * nodes, nodes))
        agg = agg + dot(hi[at], value) + dot(lo[at], value)
    agg = agg.astype(BF16)
    live = live_rows(sizes, clusters, nodes // clusters)
    mine = pl.ds(pl.multiple_of(lax.axis_index("cols") * half, half), half)

    def dense(matrix, shift, cotangent):
        pre = dot(agg, matrix) + shift
        sig = jax.nn.sigmoid(pre)
        grad = cotangent.astype(F32) * sig * (1.0 + pre * (1.0 - sig)) * live
        return pre * sig * live, grad.astype(BF16)

    hidden, grad_pre = dense(weight[...], bias[...], gout[...])
    hidden_out[...] = hidden.astype(BF16)
    sums[pl.ds(0, feats), :] = dot(agg, grad_pre, (0, 0))
    column_sums = jnp.sum(grad_pre.astype(F32), axis=0, keepdims=True)
    sums[pl.ds(feats, 8), :] = jnp.broadcast_to(column_sums, (8, column_sums.shape[1]))
    shift = pack[pl.ds(nodes + feats, 16), :].astype(F32)
    shift = shift[0:1] + shift[1:2] + shift[2:3]
    _, grad_other = dense(pack[pl.ds(nodes, feats), :], shift, pack[pl.ds(0, nodes), :])
    other_rows = pl.ds(pl.multiple_of(nodes + lax.axis_index("cols") * half, half), half)
    grad_agg = dot(weight[mine, :], grad_pre, (1, 1)) + dot(pack[other_rows, :], grad_other, (1, 1))
    grad_out_t[...] = grad_agg.astype(BF16)


def spread_kernel(levels, hi, lo, grad_t, *outs):
    value = grad_t[...]
    nodes = value.shape[1]
    for level in range(levels + 1):
        at = (slice(None), pl.ds(level * nodes, nodes))
        outs[level][...] = dot(value, hi[at]) + dot(value, lo[at])


def finish_kernel(levels, clusters, *refs):
    sizes, out = refs[0], refs[-1]
    total = refs[1][...]
    for part in refs[2:-1]:
        total = total + part[...]
    width = total.shape[1] // clusters
    node = lax.broadcasted_iota(jnp.int32, (1, width), 1)
    live = jnp.concatenate([(node < sizes[c]).astype(F32) for c in range(clusters)], axis=1)
    out[...] = (total * live).astype(BF16)


def local(features, adj_tiles, tile_src, tile_dst, tile_count, cluster_size, weight, bias, grad_out):
    clusters = cluster_size.shape[0]
    slots, width = adj_tiles.shape[:2]
    nodes, half = features.shape
    feats, hidden = weight.shape
    levels = lax.axis_size("rows").bit_length() - 1
    columns = (levels + 1) * nodes
    bias = bias.reshape(1, hidden)
    own = features.T
    other = partner(own, "cols", 0)
    hi, lo, pack = pl.pallas_call(
        functools.partial(build_kernel, levels, clusters),
        out_shape=(
            jax.ShapeDtypeStruct((nodes, columns), BF16),
            jax.ShapeDtypeStruct((nodes, columns), BF16),
            jax.ShapeDtypeStruct((nodes + feats + 16, hidden), BF16),
        ),
        in_specs=[HBM, SMEM, SMEM, SMEM, HBM, HBM, VMEM],
        out_specs=(VMEM, VMEM, VMEM),
        scratch_shapes=[
            pltpu.VMEM((nodes, columns), F32),
            pltpu.VMEM((slots, width, width), BF16),
            pltpu.SemaphoreType.DMA((-(-slots // TILE_GROUP),)),
            pltpu.SemaphoreType.DMA((2,)),
        ],
        name="build",
    )(adj_tiles, tile_src, tile_dst, tile_count, grad_out, weight, bias)
    table = pl.pallas_call(
        functools.partial(merge_kernel, clusters),
        out_shape=jax.ShapeDtypeStruct((nodes, feats), BF16),
        in_specs=[VMEM, VMEM, SMEM],
        out_specs=VMEM,
        name="merge",
    )(own, other, cluster_size)
    tables = [table] + [partner(table, "rows", bit) for bit in range(levels)]
    pack = partner(pack, "cols", 0)
    hidden_out, sums, grad_agg = pl.pallas_call(
        functools.partial(main_kernel, levels, clusters),
        out_shape=(
            jax.ShapeDtypeStruct((nodes, hidden), BF16),
            jax.ShapeDtypeStruct((feats + 8, hidden), F32),
            jax.ShapeDtypeStruct((half, nodes), BF16),
        ),
        in_specs=[VMEM] * 6 + [SMEM] + [VMEM] * (levels + 1),
        out_specs=(VMEM, VMEM, VMEM),
        name="main",
    )(hi, lo, grad_out, weight, bias, pack, cluster_size, *tables)
    parts = pl.pallas_call(
        functools.partial(spread_kernel, levels),
        out_shape=[jax.ShapeDtypeStruct((half, nodes), F32)] * (levels + 1),
        in_specs=[VMEM] * 3,
        out_specs=[VMEM] * (levels + 1),
        name="spread",
    )(hi, lo, grad_agg)
    received = [partner(parts[bit + 1], "rows", bit) for bit in range(levels)]
    for bit in range(levels):
        sums = sums + partner(sums, "rows", bit)
    grad_scale = 1.0 / math.sqrt(nodes * lax.axis_size("rows"))
    grad_features = pl.pallas_call(
        functools.partial(finish_kernel, levels, clusters),
        out_shape=jax.ShapeDtypeStruct((half, nodes), BF16),
        in_specs=[SMEM] + [VMEM] * (levels + 1),
        out_specs=VMEM,
        name="finish",
    )(cluster_size, parts[0], *received)
    return (hidden_out, sums[:feats] * grad_scale, sums[feats] * grad_scale, grad_features.T)


def solution(mesh):
    return jax.shard_map(
        local,
        mesh=mesh,
        in_specs=(
            P("rows", "cols"),
            P("rows", None, None),
            P("rows"),
            P("rows"),
            P("rows"),
            P("rows"),
            P(None, "cols"),
            P("cols"),
            P("rows", "cols"),
        ),
        out_specs=(P("rows", "cols"), P(None, "cols"), P("cols"), P("rows", "cols")),
        check_vma=False,
    )
```

```python
import functools
import math

import jax
import jax.numpy as jnp
from jax import lax
from jax.experimental import pallas as pl
from jax.experimental.pallas import tpu as pltpu
from jax.sharding import PartitionSpec as P


TILE_GROUP = 16
F32, BF16 = jnp.float32, jnp.bfloat16
VMEM = pl.BlockSpec(memory_space=pltpu.VMEM)
FAR = pl.BlockSpec(memory_space=pltpu.VMEM)
SMEM = pl.BlockSpec(memory_space=pltpu.SMEM)
HBM = pl.BlockSpec(memory_space=pl.ANY)


def partner(shard, axis, bit):
    return lax.ppermute(shard, axis, [(i, i ^ 1 << bit) for i in range(lax.axis_size(axis))])


def near(array):
    return pltpu.with_memory_space_constraint(array, pltpu.VMEM)


def kernel_call(kernel, out_shape, in_specs, args, out_specs=None, scratch=()):
    args = [near(arg) if spec is VMEM else arg for spec, arg in zip(in_specs, args, strict=True)]
    outs = jax.tree.map(lambda _: VMEM, out_shape, is_leaf=lambda x: hasattr(x, "shape"))
    return pl.pallas_call(
        kernel,
        out_shape=out_shape,
        in_specs=in_specs,
        out_specs=outs if out_specs is None else out_specs,
        scratch_shapes=list(scratch),
    )(*args)


def near_out(shape, dtype):
    return pltpu.VMEM(shape, dtype)


def dot(a, b, contract=(1, 0)):
    return lax.dot_general(
        a, b, (((contract[0],), (contract[1],)), ((), ())), preferred_element_type=F32
    )


def live_rows(sizes, clusters, width):
    node = lax.broadcasted_iota(jnp.int32, (width, 1), 0)
    return jnp.concatenate([(node < sizes[c]).astype(F32) for c in range(clusters)], axis=0)


def build_kernel(levels, clusters, tiles, src, dst, count, gout, weight, bias, hi, lo, pack, acc, held, sems, side):
    slots, width = tiles.shape[0], tiles.shape[1]
    rows, hidden = gout.shape
    feats = weight.shape[0]
    used = count[0]
    me = lax.axis_index("rows")
    starts = list(range(0, slots, TILE_GROUP))

    def fetch(first):
        size = min(TILE_GROUP, slots - first)
        return pltpu.make_async_copy(
            tiles.at[pl.ds(first, size)], held.at[pl.ds(first, size)], sems.at[first // TILE_GROUP]
        )

    for first in starts:
        @pl.when(first < used)
        def _(first=first):
            fetch(first).start()
    sides = (
        pltpu.make_async_copy(gout, pack.at[pl.ds(0, rows)], side.at[0]),
        pltpu.make_async_copy(weight, pack.at[pl.ds(rows, feats)], side.at[1]),
    )
    for copy in sides:
        copy.start()
    value = bias[...]
    top = value.astype(BF16).astype(F32)
    rest = value - top
    middle = rest.astype(BF16).astype(F32)
    row = lax.broadcasted_iota(jnp.int32, (16, hidden), 0)
    parts = jnp.where(row == 0, top, jnp.where(row == 1, middle, jnp.where(row == 2, rest - middle, 0.0)))
    pack[pl.ds(rows + feats, 16), :] = parts.astype(BF16)
    acc[...] = jnp.zeros_like(acc)

    def add(slot, carry):
        source = src[slot]
        group = lax.div(source, clusters)
        differs = jnp.bitwise_xor(group, me)
        column = source - group * clusters
        for bit in range(levels):
            column = column + jnp.where(differs == 1 << bit, (bit + 1) * clusters, 0)
        at = (
            pl.ds(pl.multiple_of(dst[slot] * width, width), width),
            pl.ds(pl.multiple_of(column * width, width), width),
        )
        acc[at] = acc[at] + held[slot].astype(F32)
        return carry

    for first in starts:
        @pl.when(first < used)
        def _(first=first):
            fetch(first).wait()
            lax.fori_loop(first, jnp.minimum(first + TILE_GROUP, used), add, 0)

    total = acc[...]
    high = total.astype(BF16)
    hi[...] = high
    lo[...] = (total - high.astype(F32)).astype(BF16)
    for copy in sides:
        copy.wait()


def merge_kernel(clusters, own, other, sizes, out):
    mine, theirs = own[...].astype(F32), other[...].astype(F32)
    first = lax.axis_index("cols") == 0
    both = jnp.concatenate(
        [jnp.where(first, mine, theirs), jnp.where(first, theirs, mine)], axis=0
    )
    live = live_rows(sizes, clusters, own.shape[1] // clusters)
    out[...] = (both.T * live).astype(BF16)


def main_kernel(levels, clusters, *refs):
    hi, lo, gout, weight, bias, pack, sizes = refs[:7]
    tables = refs[7 : 8 + levels]
    hidden_out, sums, grad_out_t, hidden_near, sem = refs[8 + levels :]
    nodes, feats = tables[0].shape
    half = grad_out_t.shape[0]
    agg = jnp.zeros((nodes, feats), F32)
    for level, table in enumerate(tables):
        value = table[...]
        at = (slice(None), pl.ds(level * nodes, nodes))
        agg = agg + dot(hi[at], value) + dot(lo[at], value)
    agg = agg.astype(BF16)
    live = live_rows(sizes, clusters, nodes // clusters)
    mine = pl.ds(pl.multiple_of(lax.axis_index("cols") * half, half), half)

    def dense(matrix, shift, cotangent):
        pre = dot(agg, matrix) + shift
        sig = jax.nn.sigmoid(pre)
        grad = cotangent.astype(F32) * sig * (1.0 + pre * (1.0 - sig)) * live
        return pre * sig * live, grad.astype(BF16)

    hidden, grad_pre = dense(weight[...], bias[...], gout[...])
    hidden_near[...] = hidden.astype(BF16)
    leave = pltpu.make_async_copy(hidden_near, hidden_out, sem)
    leave.start()
    sums[pl.ds(0, feats), :] = dot(agg, grad_pre, (0, 0))
    column_sums = jnp.sum(grad_pre.astype(F32), axis=0, keepdims=True)
    sums[pl.ds(feats, 8), :] = jnp.broadcast_to(column_sums, (8, column_sums.shape[1]))
    shift = pack[pl.ds(nodes + feats, 16), :].astype(F32)
    shift = shift[0:1] + shift[1:2] + shift[2:3]
    _, grad_other = dense(pack[pl.ds(nodes, feats), :], shift, pack[pl.ds(0, nodes), :])
    other_rows = pl.ds(pl.multiple_of(nodes + lax.axis_index("cols") * half, half), half)
    grad_agg = dot(weight[mine, :], grad_pre, (1, 1)) + dot(pack[other_rows, :], grad_other, (1, 1))
    grad_out_t[...] = grad_agg.astype(BF16)
    leave.wait()


def spread_kernel(levels, hi, lo, grad_t, *outs):
    value = grad_t[...]
    nodes = value.shape[1]
    for level in range(levels + 1):
        at = (slice(None), pl.ds(level * nodes, nodes))
        outs[level][...] = dot(value, hi[at]) + dot(value, lo[at])


def finish_kernel(clusters, *refs):
    sizes, out = refs[0], refs[-1]
    total = refs[1][...]
    for part in refs[2:-1]:
        total = total + part[...]
    width = total.shape[1] // clusters
    node = lax.broadcasted_iota(jnp.int32, (1, width), 1)
    live = jnp.concatenate([(node < sizes[c]).astype(F32) for c in range(clusters)], axis=1)
    out[...] = (total * live).astype(BF16)


def add_kernel(own, other, out):
    out[...] = own[...] + other[...]


def add(own, other):
    return kernel_call(add_kernel, near_out(own.shape, own.dtype), [VMEM, VMEM], (own, other))


def scale_kernel(scale, own, other, grad_weight, grad_bias):
    feats = grad_weight.shape[0]
    grad_weight[...] = (own[pl.ds(0, feats), :] + other[pl.ds(0, feats), :]) * scale
    grad_bias[...] = (own[pl.ds(feats, 1), :] + other[pl.ds(feats, 1), :]) * scale


def local(features, adj_tiles, tile_src, tile_dst, tile_count, cluster_size, weight, bias, grad_out):
    clusters = cluster_size.shape[0]
    slots, width = adj_tiles.shape[:2]
    nodes, half = features.shape
    feats, hidden = weight.shape
    levels = lax.axis_size("rows").bit_length() - 1
    columns = (levels + 1) * nodes
    bias = bias.reshape(1, hidden)
    own = near(features.T)
    other = partner(own, "cols", 0)
    hi, lo, pack = kernel_call(
        functools.partial(build_kernel, levels, clusters),
        (
            near_out((nodes, columns), BF16),
            near_out((nodes, columns), BF16),
            near_out((nodes + feats + 16, hidden), BF16),
        ),
        [HBM, SMEM, SMEM, SMEM, HBM, HBM, FAR],
        (adj_tiles, tile_src, tile_dst, tile_count, grad_out, weight, bias),
        scratch=[
            pltpu.VMEM((nodes, columns), F32),
            pltpu.VMEM((slots, width, width), BF16),
            pltpu.SemaphoreType.DMA((-(-slots // TILE_GROUP),)),
            pltpu.SemaphoreType.DMA((2,)),
        ],
    )
    table = kernel_call(
        functools.partial(merge_kernel, clusters),
        near_out((nodes, feats), BF16),
        [VMEM, VMEM, SMEM],
        (own, other, cluster_size),
    )
    tables = [table]
    for bit in range(levels):
        tables.append(partner(table, "rows", bit))
    pack = partner(pack, "cols", 0)
    hidden_out, sums, grad_agg = kernel_call(
        functools.partial(main_kernel, levels, clusters),
        (
            jax.ShapeDtypeStruct((nodes, hidden), BF16),
            near_out((feats + 8, hidden), F32),
            near_out((half, nodes), BF16),
        ),
        [VMEM] * 5 + [VMEM, SMEM] + [VMEM] * (levels + 1),
        (hi, lo, grad_out, weight, bias, pack, cluster_size, *tables),
        out_specs=(HBM, VMEM, VMEM),
        scratch=[pltpu.VMEM((nodes, hidden), BF16), pltpu.SemaphoreType.DMA],
    )
    parts = kernel_call(
        functools.partial(spread_kernel, levels),
        [near_out((half, nodes), F32)] * (levels + 1),
        [VMEM] * 3,
        (hi, lo, grad_agg),
    )
    received = []
    for bit in range(levels):
        received.append(partner(parts[bit + 1], "rows", bit))
    moved = None
    for bit in range(levels):
        sums = add(sums, moved) if bit else sums
        moved = partner(sums, "rows", bit)
    grad_features = kernel_call(
        functools.partial(finish_kernel, clusters),
        jax.ShapeDtypeStruct((half, nodes), BF16),
        [SMEM] + [VMEM] * (levels + 1),
        (cluster_size, parts[0], *received),
    )
    grad_scale = 1.0 / math.sqrt(nodes * lax.axis_size("rows"))
    grad_weight, grad_bias = kernel_call(
        functools.partial(scale_kernel, grad_scale),
        (jax.ShapeDtypeStruct((feats, hidden), F32), jax.ShapeDtypeStruct((1, hidden), F32)),
        [VMEM, VMEM],
        (sums, moved),
    )
    return (hidden_out, grad_weight, grad_bias.reshape(hidden), grad_features.T)


def solution(mesh):
    return jax.shard_map(
        local,
        mesh=mesh,
        in_specs=(
            P("rows", "cols"),
            P("rows", None, None),
            P("rows"),
            P("rows"),
            P("rows"),
            P("rows"),
            P(None, "cols"),
            P("cols"),
            P("rows", "cols"),
        ),
        out_specs=(P("rows", "cols"), P(None, "cols"), P("cols"), P("rows", "cols")),
        check_vma=False,
    )
```

```python
import functools
import math

import jax
import jax.numpy as jnp
from jax import lax
from jax.experimental import pallas as pl
from jax.experimental.pallas import tpu as pltpu
from jax.sharding import PartitionSpec as P


TILE_GROUP, UNROLL = 16, 4
F32, BF16 = jnp.float32, jnp.bfloat16
VMEM = pl.BlockSpec(memory_space=pltpu.VMEM)
SMEM = pl.BlockSpec(memory_space=pltpu.SMEM)
HBM = pl.BlockSpec(memory_space=pltpu.HBM)


def partner(shard, axis, bit):
    return lax.ppermute(shard, axis, [(i, i ^ 1 << bit) for i in range(lax.axis_size(axis))])


def near(array):
    return pltpu.with_memory_space_constraint(array, pltpu.VMEM)


def kernel_call(kernel, out_shape, in_specs, args, out_specs=None, scratch=()):
    args = [near(arg) if spec is VMEM else arg for spec, arg in zip(in_specs, args, strict=True)]
    outs = jax.tree.map(lambda _: VMEM, out_shape, is_leaf=lambda x: hasattr(x, "shape"))
    return pl.pallas_call(
        kernel,
        out_shape=out_shape,
        in_specs=in_specs,
        out_specs=outs if out_specs is None else out_specs,
        scratch_shapes=list(scratch),
    )(*args)


def near_out(shape, dtype):
    return pltpu.VMEM(shape, dtype)


def dot(a, b, contract=(1, 0)):
    return lax.dot_general(
        a, b, (((contract[0],), (contract[1],)), ((), ())), preferred_element_type=F32
    )


def quotient(value, divisor):
    if divisor & (divisor - 1) == 0:
        return jnp.right_shift(value, divisor.bit_length() - 1)
    return lax.div(value, divisor)


def build_kernel(levels, clusters, *refs):
    tiles, src_far, dst_far, count_far, size_far, gout, weight, bias_far, own_far = refs[:9]
    hi, lo, pack, live, live_row, own = refs[9:15]
    acc, held, src, dst, count, size, sems, bias, side = refs[15:]
    slots, width = tiles.shape[0], tiles.shape[1]
    rows, _ = gout.shape
    feats = weight.shape[0]
    columns = hi.shape[1]
    scalars = [
        pltpu.make_async_copy(far, close, side.at[n])
        for n, (far, close) in enumerate(
            ((src_far, src), (dst_far, dst), (count_far, count), (size_far, size))
        )
    ]
    for copy in scalars:
        copy.start()
    starts = list(range(0, slots, TILE_GROUP))
    fetches = [
        pltpu.make_async_copy(
            tiles.at[pl.ds(first, min(TILE_GROUP, slots - first))],
            held.at[pl.ds(first, min(TILE_GROUP, slots - first))],
            sems.at[first // TILE_GROUP],
        )
        for first in starts
    ]
    for copy in fetches:
        copy.start()
    sides = (
        pltpu.make_async_copy(gout, pack.at[pl.ds(0, rows)], side.at[4]),
        pltpu.make_async_copy(weight, pack.at[pl.ds(rows, feats)], side.at[5]),
        pltpu.make_async_copy(bias_far, bias, side.at[6]),
        pltpu.make_async_copy(own_far, own, side.at[7]),
    )
    for copy in sides:
        copy.start()
    acc[...] = jnp.zeros_like(acc)
    for copy in scalars:
        copy.wait()
    node = lax.broadcasted_iota(jnp.int32, (width, live.shape[1]), 0)
    across = lax.broadcasted_iota(jnp.int32, (live_row.shape[0], width), 1)
    for c in range(clusters):
        live[pl.ds(c * width, width), :] = (node < size[c]).astype(F32)
        live_row[:, pl.ds(c * width, width)] = (across < size[c]).astype(F32)
    used = count[0, 0]
    me = lax.axis_index("rows")

    def block_of(slot):
        at = jnp.minimum(slot, slots - 1)
        source = src[at]
        group = quotient(source, clusters)
        differs = jnp.bitwise_xor(group, me)
        column = source - group * clusters
        for bit in range(levels):
            column = column + jnp.where(differs == 1 << bit, (bit + 1) * clusters, 0)
        column = jnp.where(slot < used, column, columns // width)
        row = jnp.where(slot < used, dst[at], 0)
        return at, (
            pl.ds(pl.multiple_of(row * width, width), width),
            pl.ds(pl.multiple_of(column * width, width), width),
        )

    def step(turn, carry):
        blocks = [block_of(turn * UNROLL + k) for k in range(UNROLL)]
        for slot, block in blocks:
            acc[block] = acc[block] + held[slot].astype(F32)
        return carry

    for first, copy in zip(starts, fetches):
        copy.wait()
        last = jnp.minimum(min(first + TILE_GROUP, slots), used)
        lax.fori_loop(first // UNROLL, quotient(last + UNROLL - 1, UNROLL), step, 0)
    total = acc[:, pl.ds(0, columns)]
    high = total.astype(BF16)
    hi[...] = high
    lo[...] = (total - high.astype(F32)).astype(BF16)
    for copy in sides:
        copy.wait()
    pack[pl.ds(rows + feats, 16), :] = thirds(bias[...])


def merge_kernel(own, other, live, out):
    mine, theirs = own[...].astype(F32), other[...].astype(F32)
    first = lax.axis_index("cols") == 0
    both = jnp.concatenate(
        [jnp.where(first, mine, theirs), jnp.where(first, theirs, mine)], axis=0
    )
    out[...] = (both.T * live[...]).astype(BF16)


def dense(agg, pack, live):
    nodes, feats = agg.shape
    shift = pack[pl.ds(nodes + feats, 16), :].astype(F32)
    pre = dot(agg, pack[pl.ds(nodes, feats), :]) + (shift[0:1] + shift[1:2] + shift[2:3])
    sig = jax.nn.sigmoid(pre)
    grad = pack[pl.ds(0, nodes), :].astype(F32) * sig * (1.0 + pre * (1.0 - sig)) * live
    return pre * sig * live, grad.astype(BF16)


def thirds(value):
    top = value.astype(BF16).astype(F32)
    middle = (value - top).astype(BF16).astype(F32)
    row = lax.broadcasted_iota(jnp.int32, (16, value.shape[1]), 0)
    parts = jnp.where(row == 0, top, jnp.where(row == 1, middle, jnp.where(row == 2, value - top - middle, 0.0)))
    return parts.astype(BF16)


def main_kernel(levels, hi, lo, pack, live, *refs):
    tables = refs[: levels + 1]
    sums, agg_out, grad_pre_out, hidden_out = refs[levels + 1 :]
    nodes, feats = tables[0].shape
    agg = jnp.zeros((nodes, feats), F32)
    for level, table in enumerate(tables):
        value = table[...]
        at = (slice(None), pl.ds(level * nodes, nodes))
        agg = agg + dot(hi[at], value) + dot(lo[at], value)
    agg = agg.astype(BF16)
    hidden, grad_pre = dense(agg, pack, live[...])
    sums[pl.ds(0, feats), :] = dot(agg, grad_pre, (0, 0)).astype(BF16)
    sums[pl.ds(feats, 16), :] = thirds(jnp.sum(grad_pre.astype(F32), axis=0, keepdims=True))
    agg_out[...] = agg
    grad_pre_out[...] = grad_pre
    hidden_out[...] = hidden.astype(BF16)


def spread_kernel(levels, hi, lo, agg, grad_pre, hidden, own, pack, live, *refs):
    hidden_out, outs, sem = refs[0], refs[1:-1], refs[-1]
    leave = pltpu.make_async_copy(hidden, hidden_out, sem)
    leave.start()
    nodes, _ = agg.shape
    half = outs[0].shape[0]
    _, grad_other = dense(agg[...], pack, live[...])
    mine = pl.ds(pl.multiple_of(nodes + lax.axis_index("cols") * half, half), half)
    value = dot(own[mine, :], grad_pre[...], (1, 1)) + dot(pack[mine, :], grad_other, (1, 1))
    value = value.astype(BF16)
    for level in range(levels + 1):
        at = (slice(None), pl.ds(level * nodes, nodes))
        outs[level][...] = (dot(value, hi[at]) + dot(value, lo[at])).astype(outs[level].dtype)
    leave.wait()


def finish_kernel(live_row, *refs):
    total = refs[0][...]
    for part in refs[1:-1]:
        total = total + part[...].astype(F32)
    refs[-1][...] = (total * live_row[0:1, :]).astype(BF16)


def add_kernel(own, other, out):
    if own.dtype == F32:
        out[...] = own[...] + other[...]
    else:
        feats = own.shape[0] - 16
        total = own[...].astype(F32) + other[...].astype(F32)
        out[pl.ds(0, feats), :] = total[:feats]
        row = total[feats : feats + 1] + total[feats + 1 : feats + 2] + total[feats + 2 : feats + 3]
        out[pl.ds(feats, 8), :] = jnp.broadcast_to(row, (8, row.shape[1]))


def add(own, other):
    rows, columns = own.shape
    shape = (rows if own.dtype == F32 else rows - 8, columns)
    return kernel_call(add_kernel, near_out(shape, F32), [VMEM, VMEM], (own, other))


def scale_kernel(scale, own, other, grad_weight, grad_bias):
    feats = grad_weight.shape[0]
    grad_weight[...] = (own[pl.ds(0, feats), :] + other[pl.ds(0, feats), :]) * scale
    grad_bias[...] = (own[pl.ds(feats, 1), :] + other[pl.ds(feats, 1), :]) * scale


def local(features, adj_tiles, tile_src, tile_dst, tile_count, cluster_size, weight, bias, grad_out):
    clusters = cluster_size.shape[0]
    slots, width = adj_tiles.shape[:2]
    nodes, half = features.shape
    feats, hidden = weight.shape
    levels = lax.axis_size("rows").bit_length() - 1
    columns = (levels + 1) * nodes
    bias = bias.reshape(1, hidden)
    own = features.T
    other = partner(own, "cols", 0)
    hi, lo, pack, live, live_row, own = kernel_call(
        functools.partial(build_kernel, levels, clusters),
        (
            near_out((nodes, columns), BF16),
            near_out((nodes, columns), BF16),
            near_out((nodes + feats + 16, hidden), BF16),
            near_out((nodes, hidden), F32),
            near_out((8, nodes), F32),
            near_out((half, nodes), BF16),
        ),
        [HBM] * 9,
        (adj_tiles, tile_src, tile_dst, tile_count.reshape(1, 1), cluster_size, grad_out, weight, bias, own),
        scratch=[
            pltpu.VMEM((nodes, columns + width), F32),
            pltpu.VMEM((slots, width, width), BF16),
            pltpu.SMEM((slots,), jnp.int32),
            pltpu.SMEM((slots,), jnp.int32),
            pltpu.SMEM((1, 1), jnp.int32),
            pltpu.SMEM((clusters,), jnp.int32),
            pltpu.SemaphoreType.DMA((-(-slots // TILE_GROUP),)),
            pltpu.VMEM((1, hidden), F32),
            pltpu.SemaphoreType.DMA((8,)),
        ],
    )
    table = kernel_call(merge_kernel, near_out((nodes, feats), BF16), [VMEM, VMEM, VMEM], (own, other, live))
    tables = [table]
    for bit in range(levels):
        tables.append(partner(table, "rows", bit))
    other_pack = partner(pack, "cols", 0)
    sums, agg, grad_pre, hidden_near = kernel_call(
        functools.partial(main_kernel, levels),
        (
            near_out((feats + 16, hidden), BF16),
            near_out((nodes, feats), BF16),
            near_out((nodes, hidden), BF16),
            near_out((nodes, hidden), BF16),
        ),
        [VMEM] * (levels + 5),
        (hi, lo, pack, live, *tables),
    )
    hidden_out, *parts = kernel_call(
        functools.partial(spread_kernel, levels),
        [jax.ShapeDtypeStruct((nodes, hidden), BF16), near_out((half, nodes), F32)]
        + [near_out((half, nodes), BF16)] * levels,
        [VMEM] * 8,
        (hi, lo, agg, grad_pre, hidden_near, pack, other_pack, live),
        out_specs=[HBM] + [VMEM] * (levels + 1),
        scratch=[pltpu.SemaphoreType.DMA],
    )
    received = []
    for bit in range(levels):
        received.append(partner(parts[bit + 1], "rows", bit))
    moved = None
    for turn in range(levels):
        sums = add(sums, moved) if turn else sums
        moved = partner(sums, "rows", levels - 1 - turn)
    grad_features = kernel_call(
        finish_kernel, jax.ShapeDtypeStruct((half, nodes), BF16), [VMEM] * (levels + 2), (live_row, parts[0], *received)
    )
    grad_scale = 1.0 / math.sqrt(nodes * lax.axis_size("rows"))
    grad_weight, grad_bias = kernel_call(
        functools.partial(scale_kernel, grad_scale),
        (
            jax.ShapeDtypeStruct((feats, hidden), F32),
            jax.ShapeDtypeStruct((1, hidden), F32),
        ),
        [VMEM, VMEM],
        (sums, moved),
    )
    return (hidden_out, grad_weight, grad_bias.reshape(hidden), grad_features.T)


def solution(mesh):
    return jax.shard_map(
        local,
        mesh=mesh,
        in_specs=(
            P("rows", "cols"),
            P("rows", None, None),
            P("rows"),
            P("rows"),
            P("rows"),
            P("rows"),
            P(None, "cols"),
            P("cols"),
            P("rows", "cols"),
        ),
        out_specs=(P("rows", "cols"), P(None, "cols"), P("cols"), P("rows", "cols")),
        check_vma=False,
    )
```

```python
import functools
import math

import jax
import jax.numpy as jnp
from jax import lax
from jax.experimental import pallas as pl
from jax.experimental.pallas import tpu as pltpu
from jax.sharding import PartitionSpec as P


TILE_GROUP, UNROLL = 16, 4
F32, BF16 = jnp.float32, jnp.bfloat16
VMEM = pl.BlockSpec(memory_space=pltpu.VMEM)
SMEM = pl.BlockSpec(memory_space=pltpu.SMEM)
HBM = pl.BlockSpec(memory_space=pltpu.HBM)


def partner(shard, axis, bit):
    return lax.ppermute(shard, axis, [(i, i ^ 1 << bit) for i in range(lax.axis_size(axis))])


def near(array):
    return pltpu.with_memory_space_constraint(array, pltpu.VMEM)


def kernel_call(kernel, out_shape, in_specs, args, out_specs=None, scratch=()):
    args = [near(arg) if spec is VMEM else arg for spec, arg in zip(in_specs, args, strict=True)]
    outs = jax.tree.map(lambda _: VMEM, out_shape, is_leaf=lambda x: hasattr(x, "shape"))
    return pl.pallas_call(
        kernel,
        out_shape=out_shape,
        in_specs=in_specs,
        out_specs=outs if out_specs is None else out_specs,
        scratch_shapes=list(scratch),
    )(*args)


def near_out(shape, dtype):
    return pltpu.VMEM(shape, dtype)


def dot(a, b, contract=(1, 0)):
    return lax.dot_general(
        a, b, (((contract[0],), (contract[1],)), ((), ())), preferred_element_type=F32
    )


def quotient(value, divisor):
    if divisor & (divisor - 1) == 0:
        return jnp.right_shift(value, divisor.bit_length() - 1)
    return lax.div(value, divisor)


def build_kernel(levels, clusters, *refs):
    tiles, src_far, dst_far, count_far, size_far, gout, weight, bias_far, own_far = refs[:9]
    hi, lo, pack, live, live_row, own = refs[9:15]
    acc, held, src, dst, count, size, sems, bias, side = refs[15:]
    slots, width = tiles.shape[0], tiles.shape[1]
    rows, _ = gout.shape
    feats = weight.shape[0]
    columns = hi.shape[1]
    scalars = [
        pltpu.make_async_copy(far, close, side.at[n])
        for n, (far, close) in enumerate(
            ((src_far, src), (dst_far, dst), (count_far, count), (size_far, size))
        )
    ]
    for copy in scalars:
        copy.start()
    starts = list(range(0, slots, TILE_GROUP))
    fetches = [
        pltpu.make_async_copy(
            tiles.at[pl.ds(first, min(TILE_GROUP, slots - first))],
            held.at[pl.ds(first, min(TILE_GROUP, slots - first))],
            sems.at[first // TILE_GROUP],
        )
        for first in starts
    ]
    for copy in fetches:
        copy.start()
    sides = (
        pltpu.make_async_copy(gout, pack.at[pl.ds(0, rows)], side.at[4]),
        pltpu.make_async_copy(weight, pack.at[pl.ds(rows, feats)], side.at[5]),
        pltpu.make_async_copy(bias_far, bias, side.at[6]),
        pltpu.make_async_copy(own_far, own, side.at[7]),
    )
    for copy in sides:
        copy.start()
    acc[...] = jnp.zeros_like(acc)
    for copy in scalars:
        copy.wait()
    node = lax.broadcasted_iota(jnp.int32, (width, live.shape[1]), 0)
    across = lax.broadcasted_iota(jnp.int32, (live_row.shape[0], width), 1)
    for c in range(clusters):
        live[pl.ds(c * width, width), :] = (node < size[c]).astype(F32)
        live_row[:, pl.ds(c * width, width)] = (across < size[c]).astype(F32)
    used = count[0, 0]
    me = lax.axis_index("rows")

    def block_of(slot):
        at = jnp.minimum(slot, slots - 1)
        source = src[at]
        group = quotient(source, clusters)
        differs = jnp.bitwise_xor(group, me)
        column = source - group * clusters
        for bit in range(levels):
            column = column + jnp.where(differs == 1 << bit, (bit + 1) * clusters, 0)
        column = jnp.where(slot < used, column, columns // width)
        row = jnp.where(slot < used, dst[at], 0)
        return at, (
            pl.ds(pl.multiple_of(row * width, width), width),
            pl.ds(pl.multiple_of(column * width, width), width),
        )

    def step(turn, carry):
        blocks = [block_of(turn * UNROLL + k) for k in range(UNROLL)]
        for slot, block in blocks:
            acc[block] = acc[block] + held[slot].astype(F32)
        return carry

    for first, copy in zip(starts, fetches):
        copy.wait()
        last = jnp.minimum(min(first + TILE_GROUP, slots), used)
        lax.fori_loop(first // UNROLL, quotient(last + UNROLL - 1, UNROLL), step, 0)
    total = acc[:, pl.ds(0, columns)]
    high = total.astype(BF16)
    hi[...] = high
    lo[...] = (total - high.astype(F32)).astype(BF16)
    for copy in sides:
        copy.wait()
    pack[pl.ds(rows + feats, 16), :] = thirds(bias[...])


def merge_kernel(own, other, live, out):
    mine, theirs = own[...].astype(F32), other[...].astype(F32)
    first = lax.axis_index("cols") == 0
    both = jnp.concatenate(
        [jnp.where(first, mine, theirs), jnp.where(first, theirs, mine)], axis=0
    )
    out[...] = (both.T * live[...]).astype(BF16)


def dense(agg, pack, live):
    nodes, feats = agg.shape
    shift = pack[pl.ds(nodes + feats, 16), :].astype(F32)
    pre = dot(agg, pack[pl.ds(nodes, feats), :]) + (shift[0:1] + shift[1:2] + shift[2:3])
    sig = jax.nn.sigmoid(pre)
    grad = pack[pl.ds(0, nodes), :].astype(F32) * sig * (1.0 + pre * (1.0 - sig)) * live
    return pre * sig * live, grad.astype(BF16)


def thirds(value):
    top = value.astype(BF16).astype(F32)
    middle = (value - top).astype(BF16).astype(F32)
    row = lax.broadcasted_iota(jnp.int32, (16, value.shape[1]), 0)
    parts = jnp.where(row == 0, top, jnp.where(row == 1, middle, jnp.where(row == 2, value - top - middle, 0.0)))
    return parts.astype(BF16)


def main_kernel(levels, hi, lo, pack, live, *refs):
    tables = refs[: levels + 1]
    sums, agg_out, grad_pre_out, hidden_out = refs[levels + 1 :]
    nodes, feats = tables[0].shape
    agg = jnp.zeros((nodes, feats), F32)
    for level, table in enumerate(tables):
        value = table[...]
        at = (slice(None), pl.ds(level * nodes, nodes))
        agg = agg + dot(hi[at], value) + dot(lo[at], value)
    agg = agg.astype(BF16)
    hidden, grad_pre = dense(agg, pack, live[...])
    sums[pl.ds(0, feats), :] = dot(agg, grad_pre, (0, 0)).astype(BF16)
    sums[pl.ds(feats, 16), :] = thirds(jnp.sum(grad_pre.astype(F32), axis=0, keepdims=True))
    agg_out[...] = agg
    grad_pre_out[...] = grad_pre
    hidden_out[...] = hidden.astype(BF16)


def spread_kernel(levels, hi, lo, agg, grad_pre, hidden, own, pack, live, *refs):
    hidden_out, outs, sem = refs[0], refs[1:-1], refs[-1]
    leave = pltpu.make_async_copy(hidden, hidden_out, sem)
    leave.start()
    nodes, _ = agg.shape
    half = outs[0].shape[0]
    _, grad_other = dense(agg[...], pack, live[...])
    mine = pl.ds(pl.multiple_of(nodes + lax.axis_index("cols") * half, half), half)
    value = dot(own[mine, :], grad_pre[...], (1, 1)) + dot(pack[mine, :], grad_other, (1, 1))
    value = value.astype(BF16)
    for level in range(levels + 1):
        at = (slice(None), pl.ds(level * nodes, nodes))
        outs[level][...] = (dot(value, hi[at]) + dot(value, lo[at])).astype(outs[level].dtype)
    leave.wait()


def finish_kernel(live_row, *refs):
    total = refs[0][...]
    for part in refs[1:-1]:
        total = total + part[...].astype(F32)
    refs[-1][...] = (total * live_row[0:1, :]).astype(BF16)


def add_kernel(own, other, out):
    feats = own.shape[0] - 16
    total = own[...].astype(F32) + other[...].astype(F32)
    row = total[feats : feats + 1] + total[feats + 1 : feats + 2] + total[feats + 2 : feats + 3]
    out[pl.ds(0, feats), :] = total[:feats].astype(out.dtype)
    if out.dtype == F32:
        out[pl.ds(feats, 8), :] = jnp.broadcast_to(row, (8, row.shape[1]))
    else:
        out[pl.ds(feats, 16), :] = thirds(row)


def add(own, other, dtype):
    rows, columns = own.shape
    shape = (rows - 8 if dtype == F32 else rows, columns)
    return kernel_call(add_kernel, near_out(shape, dtype), [VMEM, VMEM], (own, other))


def scale_kernel(scale, own, other, grad_weight, grad_bias):
    feats = grad_weight.shape[0]
    grad_weight[...] = (own[pl.ds(0, feats), :] + other[pl.ds(0, feats), :]) * scale
    grad_bias[...] = (own[pl.ds(feats, 1), :] + other[pl.ds(feats, 1), :]) * scale


def local(features, adj_tiles, tile_src, tile_dst, tile_count, cluster_size, weight, bias, grad_out):
    clusters = cluster_size.shape[0]
    slots, width = adj_tiles.shape[:2]
    nodes, half = features.shape
    feats, hidden = weight.shape
    levels = lax.axis_size("rows").bit_length() - 1
    columns = (levels + 1) * nodes
    bias = bias.reshape(1, hidden)
    own = features.T
    other = partner(own, "cols", 0)
    hi, lo, pack, live, live_row, own = kernel_call(
        functools.partial(build_kernel, levels, clusters),
        (
            near_out((nodes, columns), BF16),
            near_out((nodes, columns), BF16),
            near_out((nodes + feats + 16, hidden), BF16),
            near_out((nodes, hidden), F32),
            near_out((8, nodes), F32),
            near_out((half, nodes), BF16),
        ),
        [HBM] * 9,
        (adj_tiles, tile_src, tile_dst, tile_count.reshape(1, 1), cluster_size, grad_out, weight, bias, own),
        scratch=[
            pltpu.VMEM((nodes, columns + width), F32),
            pltpu.VMEM((slots, width, width), BF16),
            pltpu.SMEM((slots,), jnp.int32),
            pltpu.SMEM((slots,), jnp.int32),
            pltpu.SMEM((1, 1), jnp.int32),
            pltpu.SMEM((clusters,), jnp.int32),
            pltpu.SemaphoreType.DMA((-(-slots // TILE_GROUP),)),
            pltpu.VMEM((1, hidden), F32),
            pltpu.SemaphoreType.DMA((8,)),
        ],
    )
    table = kernel_call(merge_kernel, near_out((nodes, feats), BF16), [VMEM, VMEM, VMEM], (own, other, live))
    tables = [table]
    for bit in range(levels):
        tables.append(partner(table, "rows", bit))
    other_pack = partner(pack, "cols", 0)
    sums, agg, grad_pre, hidden_near = kernel_call(
        functools.partial(main_kernel, levels),
        (
            near_out((feats + 16, hidden), BF16),
            near_out((nodes, feats), BF16),
            near_out((nodes, hidden), BF16),
            near_out((nodes, hidden), BF16),
        ),
        [VMEM] * (levels + 5),
        (hi, lo, pack, live, *tables),
    )
    hidden_out, *parts = kernel_call(
        functools.partial(spread_kernel, levels),
        [jax.ShapeDtypeStruct((nodes, hidden), BF16), near_out((half, nodes), F32)]
        + [near_out((half, nodes), BF16)] * levels,
        [VMEM] * 8,
        (hi, lo, agg, grad_pre, hidden_near, pack, other_pack, live),
        out_specs=[HBM] + [VMEM] * (levels + 1),
        scratch=[pltpu.SemaphoreType.DMA],
    )
    received = []
    for bit in range(levels):
        received.append(partner(parts[bit + 1], "rows", bit))
    moved = None
    for turn in range(levels):
        if turn:
            sums = add(sums, moved, F32 if turn + 1 == levels else BF16)
        moved = partner(sums, "rows", sum_bits(levels)[turn])
    grad_features = kernel_call(
        finish_kernel, jax.ShapeDtypeStruct((half, nodes), BF16), [VMEM] * (levels + 2), (live_row, parts[0], *received)
    )
    grad_scale = 1.0 / math.sqrt(nodes * lax.axis_size("rows"))
    grad_weight, grad_bias = kernel_call(
        functools.partial(scale_kernel, grad_scale),
        (
            jax.ShapeDtypeStruct((feats, hidden), F32),
            jax.ShapeDtypeStruct((1, hidden), F32),
        ),
        [VMEM, VMEM],
        (sums, moved),
    )
    return (hidden_out, grad_weight, grad_bias.reshape(hidden), grad_features.T)


def sum_bits(levels):
    return list(reversed(range(levels)))


def solution(mesh):
    return jax.shard_map(
        local,
        mesh=mesh,
        in_specs=(
            P("rows", "cols"),
            P("rows", None, None),
            P("rows"),
            P("rows"),
            P("rows"),
            P("rows"),
            P(None, "cols"),
            P("cols"),
            P("rows", "cols"),
        ),
        out_specs=(P("rows", "cols"), P(None, "cols"), P("cols"), P("rows", "cols")),
        check_vma=False,
    )
```

```python
import functools
import math

import jax
import jax.numpy as jnp
from jax import lax
from jax.experimental import pallas as pl
from jax.experimental.pallas import tpu as pltpu
from jax.sharding import PartitionSpec as P


TILE_GROUP, UNROLL = 16, 4
F32, BF16 = jnp.float32, jnp.bfloat16
VMEM = pl.BlockSpec(memory_space=pltpu.VMEM)
SMEM = pl.BlockSpec(memory_space=pltpu.SMEM)
HBM = pl.BlockSpec(memory_space=pltpu.HBM)


def partner(shard, axis, bit):
    return lax.ppermute(shard, axis, [(i, i ^ 1 << bit) for i in range(lax.axis_size(axis))])


def near(array):
    return pltpu.with_memory_space_constraint(array, pltpu.VMEM)


def kernel_call(kernel, out_shape, in_specs, args, out_specs=None, scratch=()):
    args = [near(arg) if spec is VMEM else arg for spec, arg in zip(in_specs, args, strict=True)]
    outs = jax.tree.map(lambda _: VMEM, out_shape, is_leaf=lambda x: hasattr(x, "shape"))
    return pl.pallas_call(
        kernel,
        out_shape=out_shape,
        in_specs=in_specs,
        out_specs=outs if out_specs is None else out_specs,
        scratch_shapes=list(scratch),
    )(*args)


def near_out(shape, dtype):
    return pltpu.VMEM(shape, dtype)


def dot(a, b, contract=(1, 0)):
    return lax.dot_general(
        a, b, (((contract[0],), (contract[1],)), ((), ())), preferred_element_type=F32
    )


def quotient(value, divisor):
    if divisor & (divisor - 1) == 0:
        return jnp.right_shift(value, divisor.bit_length() - 1)
    return lax.div(value, divisor)


def prepare_kernel(clusters, *refs):
    size_far, gout, weight, bias_far, own_far = refs[:5]
    pack, live, live_row, own = refs[5:9]
    size, bias, sems = refs[9:]
    rows = gout.shape[0]
    feats = weight.shape[0]
    width = rows // clusters
    copies = [
        pltpu.make_async_copy(far, close, sems.at[n])
        for n, (far, close) in enumerate(
            (
                (size_far, size),
                (bias_far, bias),
                (own_far, own),
                (weight, pack.at[pl.ds(rows, feats)]),
                (gout, pack.at[pl.ds(0, rows)]),
            )
        )
    ]
    for copy in copies:
        copy.start()
    for copy in copies[:2]:
        copy.wait()
    pack[pl.ds(rows + feats, 16), :] = thirds(bias[...])
    node = lax.broadcasted_iota(jnp.int32, (width, live.shape[1]), 0)
    across = lax.broadcasted_iota(jnp.int32, (live_row.shape[0], width), 1)
    for c in range(clusters):
        live[pl.ds(c * width, width), :] = (node < size[c]).astype(F32)
        live_row[:, pl.ds(c * width, width)] = (across < size[c]).astype(F32)
    for copy in copies[2:]:
        copy.wait()


def count_kernel(count, out):
    out[...] = jnp.full_like(out, count[0])


def build_kernel(levels, clusters, *refs):
    tiles, src_far, dst_far, count_far, hi, lo, acc, held, src, dst, count, sems, side = refs
    slots, width = tiles.shape[0], tiles.shape[1]
    columns = hi.shape[1]
    scalars = [
        pltpu.make_async_copy(far, close, side.at[n])
        for n, (far, close) in enumerate(((src_far, src), (dst_far, dst), (count_far, count)))
    ]
    for copy in scalars:
        copy.start()
    starts = list(range(0, slots, TILE_GROUP))
    fetches = [
        pltpu.make_async_copy(
            tiles.at[pl.ds(first, min(TILE_GROUP, slots - first))],
            held.at[pl.ds(first, min(TILE_GROUP, slots - first))],
            sems.at[first // TILE_GROUP],
        )
        for first in starts
    ]
    for copy in fetches:
        copy.start()
    acc[...] = jnp.zeros_like(acc)
    for copy in scalars:
        copy.wait()
    used = count[0, 0]
    me = lax.axis_index("rows")

    def block_of(slot):
        at = jnp.minimum(slot, slots - 1)
        source = src[at]
        group = quotient(source, clusters)
        differs = jnp.bitwise_xor(group, me)
        column = source - group * clusters
        for bit in range(levels):
            column = column + jnp.where(differs == 1 << bit, (bit + 1) * clusters, 0)
        column = jnp.where(slot < used, column, columns // width)
        row = jnp.where(slot < used, dst[at], 0)
        return at, (
            pl.ds(pl.multiple_of(row * width, width), width),
            pl.ds(pl.multiple_of(column * width, width), width),
        )

    def step(turn, carry):
        blocks = [block_of(turn * UNROLL + k) for k in range(UNROLL)]
        for slot, block in blocks:
            acc[block] = acc[block] + held[slot].astype(F32)
        return carry

    for first, copy in zip(starts, fetches):
        copy.wait()
        last = jnp.minimum(min(first + TILE_GROUP, slots), used)
        lax.fori_loop(first // UNROLL, quotient(last + UNROLL - 1, UNROLL), step, 0)
    total = acc[:, pl.ds(0, columns)]
    high = total.astype(BF16)
    hi[...] = high
    lo[...] = (total - high.astype(F32)).astype(BF16)


def merge_kernel(own, other, live, out):
    mine, theirs = own[...].astype(F32), other[...].astype(F32)
    first = lax.axis_index("cols") == 0
    both = jnp.concatenate(
        [jnp.where(first, mine, theirs), jnp.where(first, theirs, mine)], axis=0
    )
    out[...] = (both.T * live[...]).astype(BF16)


def dense(agg, pack, live):
    nodes, feats = agg.shape
    shift = pack[pl.ds(nodes + feats, 16), :].astype(F32)
    pre = dot(agg, pack[pl.ds(nodes, feats), :]) + (shift[0:1] + shift[1:2] + shift[2:3])
    sig = jax.nn.sigmoid(pre)
    grad = pack[pl.ds(0, nodes), :].astype(F32) * sig * (1.0 + pre * (1.0 - sig)) * live
    return pre * sig * live, grad.astype(BF16)


def thirds(value):
    top = value.astype(BF16).astype(F32)
    middle = (value - top).astype(BF16).astype(F32)
    row = lax.broadcasted_iota(jnp.int32, (16, value.shape[1]), 0)
    parts = jnp.where(row == 0, top, jnp.where(row == 1, middle, jnp.where(row == 2, value - top - middle, 0.0)))
    return parts.astype(BF16)


def main_kernel(levels, hi, lo, pack, live, *refs):
    tables = refs[: levels + 1]
    sums, agg_out, grad_pre_out, hidden_out = refs[levels + 1 :]
    nodes, feats = tables[0].shape
    agg = jnp.zeros((nodes, feats), F32)
    for level, table in enumerate(tables):
        value = table[...]
        at = (slice(None), pl.ds(level * nodes, nodes))
        agg = agg + dot(hi[at], value) + dot(lo[at], value)
    agg = agg.astype(BF16)
    hidden, grad_pre = dense(agg, pack, live[...])
    sums[pl.ds(0, feats), :] = dot(agg, grad_pre, (0, 0)).astype(BF16)
    sums[pl.ds(feats, 16), :] = thirds(jnp.sum(grad_pre.astype(F32), axis=0, keepdims=True))
    agg_out[...] = agg
    grad_pre_out[...] = grad_pre
    hidden_out[...] = hidden.astype(BF16)


def spread_kernel(levels, hi, lo, agg, grad_pre, hidden, own, pack, live, *refs):
    hidden_out, outs, sem = refs[0], refs[1:-1], refs[-1]
    leave = pltpu.make_async_copy(hidden, hidden_out, sem)
    leave.start()
    nodes, _ = agg.shape
    half = outs[0].shape[0]
    _, grad_other = dense(agg[...], pack, live[...])
    mine = pl.ds(pl.multiple_of(nodes + lax.axis_index("cols") * half, half), half)
    value = dot(own[mine, :], grad_pre[...], (1, 1)) + dot(pack[mine, :], grad_other, (1, 1))
    value = value.astype(BF16)
    for level in range(levels + 1):
        at = (slice(None), pl.ds(level * nodes, nodes))
        part = dot(value, hi[at]) + dot(value, lo[at])
        outs[level][...] = part.astype(outs[level].dtype)
    leave.wait()


def add_kernel(own, other, out):
    feats = own.shape[0] - 16
    total = own[...].astype(F32) + other[...].astype(F32)
    row = total[feats : feats + 1] + total[feats + 1 : feats + 2] + total[feats + 2 : feats + 3]
    out[pl.ds(0, feats), :] = total[:feats].astype(out.dtype)
    if out.dtype == F32:
        out[pl.ds(feats, 8), :] = jnp.broadcast_to(row, (8, row.shape[1]))
    else:
        out[pl.ds(feats, 16), :] = thirds(row)


def add(own, other, dtype):
    rows, columns = own.shape
    shape = (rows - 8 if dtype == F32 else rows, columns)
    return kernel_call(add_kernel, near_out(shape, dtype), [VMEM, VMEM], (own, other))


def finish_kernel(scale, own, other, live_row, *refs):
    parts, (grad_weight, grad_bias, grad_features) = refs[:-3], refs[-3:]
    feats = grad_weight.shape[0]
    grad_weight[...] = (own[pl.ds(0, feats), :] + other[pl.ds(0, feats), :]) * scale
    grad_bias[...] = (own[pl.ds(feats, 1), :] + other[pl.ds(feats, 1), :]) * scale
    total = parts[0][...]
    for part in parts[1:]:
        total = total + part[...].astype(F32)
    grad_features[...] = (total * live_row[0:1, :]).astype(BF16)


def local(features, adj_tiles, tile_src, tile_dst, tile_count, cluster_size, weight, bias, grad_out):
    clusters = cluster_size.shape[0]
    slots, width = adj_tiles.shape[:2]
    nodes, half = features.shape
    feats, hidden = weight.shape
    levels = lax.axis_size("rows").bit_length() - 1
    columns = (levels + 1) * nodes
    bias = bias.reshape(1, hidden)
    own = features.T
    other = partner(own, "cols", 0)
    pack, live, live_row, own = kernel_call(
        functools.partial(prepare_kernel, clusters),
        (
            near_out((nodes + feats + 16, hidden), BF16),
            near_out((nodes, hidden), F32),
            near_out((8, nodes), F32),
            near_out((half, nodes), BF16),
        ),
        [HBM] * 5,
        (cluster_size, grad_out, weight, bias, own),
        scratch=[pltpu.SMEM((clusters,), jnp.int32), pltpu.VMEM((1, hidden), F32), pltpu.SemaphoreType.DMA((5,))],
    )
    used = kernel_call(count_kernel, near_out((8, hidden), jnp.int32), [SMEM], (tile_count,))
    hi, lo = kernel_call(
        functools.partial(build_kernel, levels, clusters),
        (near_out((nodes, columns), BF16), near_out((nodes, columns), BF16)),
        [HBM] * 3 + [VMEM],
        (adj_tiles, tile_src, tile_dst, used),
        scratch=[
            pltpu.VMEM((nodes, columns + width), F32),
            pltpu.VMEM((slots, width, width), BF16),
            pltpu.SMEM((slots,), jnp.int32),
            pltpu.SMEM((slots,), jnp.int32),
            pltpu.SMEM((8, hidden), jnp.int32),
            pltpu.SemaphoreType.DMA((-(-slots // TILE_GROUP),)),
            pltpu.SemaphoreType.DMA((3,)),
        ],
    )
    table = kernel_call(merge_kernel, near_out((nodes, feats), BF16), [VMEM, VMEM, VMEM], (own, other, live))
    tables = [table]
    for bit in range(levels):
        tables.append(partner(table, "rows", bit))
    other_pack = partner(pack, "cols", 0)
    sums, agg, grad_pre, hidden_near = kernel_call(
        functools.partial(main_kernel, levels),
        (
            near_out((feats + 16, hidden), BF16),
            near_out((nodes, feats), BF16),
            near_out((nodes, hidden), BF16),
            near_out((nodes, hidden), BF16),
        ),
        [VMEM] * (levels + 5),
        (hi, lo, pack, live, *tables),
    )
    hidden_out, stays, *parts = kernel_call(
        functools.partial(spread_kernel, levels),
        [jax.ShapeDtypeStruct((nodes, hidden), BF16), near_out((half, nodes), F32)]
        + [near_out((half, nodes), BF16)] * levels,
        [VMEM] * 8,
        (hi, lo, agg, grad_pre, hidden_near, pack, other_pack, live),
        out_specs=[HBM] + [VMEM] * (levels + 1),
        scratch=[pltpu.SemaphoreType.DMA],
    )
    received = []
    for bit in range(levels):
        received.append(partner(parts[bit], "rows", bit))
    moved = None
    for turn, bit in enumerate(sum_bits(levels)):
        if turn:
            sums = add(sums, moved, F32 if turn + 1 == levels else BF16)
        moved = partner(sums, "rows", bit)
    grad_scale = 1.0 / math.sqrt(nodes * lax.axis_size("rows"))
    grad_weight, grad_bias, grad_features = kernel_call(
        functools.partial(finish_kernel, grad_scale),
        (
            jax.ShapeDtypeStruct((feats, hidden), F32),
            jax.ShapeDtypeStruct((1, hidden), F32),
            jax.ShapeDtypeStruct((half, nodes), BF16),
        ),
        [VMEM] * (levels + 4),
        (sums, moved, live_row, stays, *received),
    )
    return (hidden_out, grad_weight, grad_bias.reshape(hidden), grad_features.T)


def sum_bits(levels):
    return list(reversed(range(levels)))


def solution(mesh):
    return jax.shard_map(
        local,
        mesh=mesh,
        in_specs=(
            P("rows", "cols"),
            P("rows", None, None),
            P("rows"),
            P("rows"),
            P("rows"),
            P("rows"),
            P(None, "cols"),
            P("cols"),
            P("rows", "cols"),
        ),
        out_specs=(P("rows", "cols"), P(None, "cols"), P("cols"), P("rows", "cols")),
        check_vma=False,
    )
```

```python
import functools
import math

import jax
import jax.numpy as jnp
from jax import lax
from jax.experimental import pallas as pl
from jax.experimental.pallas import tpu as pltpu
from jax.sharding import PartitionSpec as P


TILE_GROUP, UNROLL = 16, 4
F32, BF16 = jnp.float32, jnp.bfloat16
VMEM = pl.BlockSpec(memory_space=pltpu.VMEM)
SMEM = pl.BlockSpec(memory_space=pltpu.SMEM)
HBM = pl.BlockSpec(memory_space=pltpu.HBM)


def partner(shard, axis, mask):
    return lax.ppermute(shard, axis, [(i, i ^ mask) for i in range(lax.axis_size(axis))])


def near(array):
    return pltpu.with_memory_space_constraint(array, pltpu.VMEM)


def kernel_call(kernel, out_shape, in_specs, args, out_specs=None, scratch=()):
    args = [near(arg) if spec is VMEM else arg for spec, arg in zip(in_specs, args, strict=True)]
    outs = jax.tree.map(lambda _: VMEM, out_shape, is_leaf=lambda x: hasattr(x, "shape"))
    return pl.pallas_call(
        kernel,
        out_shape=out_shape,
        in_specs=in_specs,
        out_specs=outs if out_specs is None else out_specs,
        scratch_shapes=list(scratch),
    )(*args)


def near_out(shape, dtype):
    return pltpu.VMEM(shape, dtype)


def dot(a, b, contract=(1, 0)):
    return lax.dot_general(
        a, b, (((contract[0],), (contract[1],)), ((), ())), preferred_element_type=F32
    )


def quotient(value, divisor):
    if divisor & (divisor - 1) == 0:
        return jnp.right_shift(value, divisor.bit_length() - 1)
    return lax.div(value, divisor)


def prepare_kernel(clusters, *refs):
    size_far, gout, weight, bias_far, own_far = refs[:5]
    pack, live, live_row, own = refs[5:9]
    size, bias, sems = refs[9:]
    rows = gout.shape[0]
    feats = weight.shape[0]
    width = rows // clusters
    copies = [
        pltpu.make_async_copy(far, close, sems.at[n])
        for n, (far, close) in enumerate(
            (
                (size_far, size),
                (bias_far, bias),
                (own_far, own),
                (weight, pack.at[pl.ds(rows, feats)]),
                (gout, pack.at[pl.ds(0, rows)]),
            )
        )
    ]
    for copy in copies:
        copy.start()
    for copy in copies[:2]:
        copy.wait()
    pack[pl.ds(rows + feats, 16), :] = thirds(bias[...])
    node = lax.broadcasted_iota(jnp.int32, (width, live.shape[1]), 0)
    across = lax.broadcasted_iota(jnp.int32, (live_row.shape[0], width), 1)
    for c in range(clusters):
        live[pl.ds(c * width, width), :] = (node < size[c]).astype(F32)
        live_row[:, pl.ds(c * width, width)] = (across < size[c]).astype(F32)
    for copy in copies[2:]:
        copy.wait()


def count_kernel(count, out):
    out[...] = jnp.full_like(out, count[0])


def build_kernel(levels, clusters, *refs):
    tiles, src_far, dst_far, count_far, hi, lo, acc, held, src, dst, count, sems, side = refs
    slots, width = tiles.shape[0], tiles.shape[1]
    columns = hi.shape[1]
    scalars = [
        pltpu.make_async_copy(far, close, side.at[n])
        for n, (far, close) in enumerate(((src_far, src), (dst_far, dst), (count_far, count)))
    ]
    for copy in scalars:
        copy.start()
    starts = list(range(0, slots, TILE_GROUP))
    fetches = [
        pltpu.make_async_copy(
            tiles.at[pl.ds(first, min(TILE_GROUP, slots - first))],
            held.at[pl.ds(first, min(TILE_GROUP, slots - first))],
            sems.at[first // TILE_GROUP],
        )
        for first in starts
    ]
    for copy in fetches:
        copy.start()
    acc[...] = jnp.zeros_like(acc)
    for copy in scalars:
        copy.wait()
    used = count[0, 0]
    me = lax.axis_index("rows")

    def block_of(slot):
        at = jnp.minimum(slot, slots - 1)
        source = src[at]
        group = quotient(source, clusters)
        differs = jnp.bitwise_xor(group, me)
        column = source - group * clusters
        for bit in range(levels):
            column = column + jnp.where(differs == 1 << bit, (bit + 1) * clusters, 0)
        column = jnp.where(slot < used, column, columns // width)
        row = jnp.where(slot < used, dst[at], 0)
        return at, (
            pl.ds(pl.multiple_of(row * width, width), width),
            pl.ds(pl.multiple_of(column * width, width), width),
        )

    def step(turn, carry):
        blocks = [block_of(turn * UNROLL + k) for k in range(UNROLL)]
        for slot, block in blocks:
            acc[block] = acc[block] + held[slot].astype(F32)
        return carry

    for first, copy in zip(starts, fetches):
        copy.wait()
        last = jnp.minimum(min(first + TILE_GROUP, slots), used)
        lax.fori_loop(first // UNROLL, quotient(last + UNROLL - 1, UNROLL), step, 0)
    total = acc[:, pl.ds(0, columns)]
    high = total.astype(BF16)
    hi[...] = high
    lo[...] = (total - high.astype(F32)).astype(BF16)


def merge_kernel(own, other, live, out):
    mine, theirs = own[...].astype(F32), other[...].astype(F32)
    first = lax.axis_index("cols") == 0
    both = jnp.concatenate(
        [jnp.where(first, mine, theirs), jnp.where(first, theirs, mine)], axis=0
    )
    out[...] = (both.T * live[...]).astype(BF16)


def dense(agg, pack, live):
    nodes, feats = agg.shape
    shift = pack[pl.ds(nodes + feats, 16), :].astype(F32)
    pre = dot(agg, pack[pl.ds(nodes, feats), :]) + (shift[0:1] + shift[1:2] + shift[2:3])
    sig = jax.nn.sigmoid(pre)
    grad = pack[pl.ds(0, nodes), :].astype(F32) * sig * (1.0 + pre * (1.0 - sig)) * live
    return pre * sig * live, grad.astype(BF16)


def thirds(value):
    top = value.astype(BF16).astype(F32)
    middle = (value - top).astype(BF16).astype(F32)
    row = lax.broadcasted_iota(jnp.int32, (16, value.shape[1]), 0)
    parts = jnp.where(row == 0, top, jnp.where(row == 1, middle, jnp.where(row == 2, value - top - middle, 0.0)))
    return parts.astype(BF16)


def main_kernel(levels, hi, lo, pack, live, *refs):
    tables = refs[: levels + 1]
    sums, agg_out, grad_pre_out, hidden_out = refs[levels + 1 :]
    nodes, feats = tables[0].shape
    agg = jnp.zeros((nodes, feats), F32)
    for level, table in enumerate(tables):
        value = table[...]
        at = (slice(None), pl.ds(level * nodes, nodes))
        agg = agg + dot(hi[at], value) + dot(lo[at], value)
    agg = agg.astype(BF16)
    hidden, grad_pre = dense(agg, pack, live[...])
    sums[pl.ds(0, feats), :] = dot(agg, grad_pre, (0, 0)).astype(BF16)
    sums[pl.ds(feats, 16), :] = thirds(jnp.sum(grad_pre.astype(F32), axis=0, keepdims=True))
    agg_out[...] = agg
    grad_pre_out[...] = grad_pre
    hidden_out[...] = hidden.astype(BF16)


def spread_kernel(levels, hi, lo, agg, grad_pre, hidden, own, pack, live, *refs):
    hidden_out, outs, sem = refs[0], refs[1:-1], refs[-1]
    leave = pltpu.make_async_copy(hidden, hidden_out, sem)
    leave.start()
    nodes, _ = agg.shape
    half = outs[0].shape[0]
    _, grad_other = dense(agg[...], pack, live[...])
    mine = pl.ds(pl.multiple_of(nodes + lax.axis_index("cols") * half, half), half)
    value = dot(own[mine, :], grad_pre[...], (1, 1)) + dot(pack[mine, :], grad_other, (1, 1))
    value = value.astype(BF16)
    for level in range(levels + 1):
        at = (slice(None), pl.ds(level * nodes, nodes))
        part = dot(value, hi[at]) + dot(value, lo[at])
        outs[level][...] = part.astype(outs[level].dtype)
    leave.wait()


def add_kernel(*refs):
    shares, out = [ref[...].astype(F32) for ref in refs[:-1]], refs[-1]
    feats = shares[0].shape[0] - 16
    while len(shares) > 1:
        shares = [a + b for a, b in zip(shares[::2], shares[1::2])]
    total = shares[0]
    row = total[feats : feats + 1] + total[feats + 1 : feats + 2] + total[feats + 2 : feats + 3]
    out[pl.ds(0, feats), :] = total[:feats].astype(out.dtype)
    if out.dtype == F32:
        out[pl.ds(feats, 8), :] = jnp.broadcast_to(row, (8, row.shape[1]))
    else:
        out[pl.ds(feats, 16), :] = thirds(row)


def add(shares, dtype):
    rows, columns = shares[0].shape
    shape = (rows - 8 if dtype == F32 else rows, columns)
    return kernel_call(add_kernel, near_out(shape, dtype), [VMEM] * len(shares), shares)


def finish_kernel(scale, own, other, live_row, *refs):
    parts, (grad_weight, grad_bias, grad_features) = refs[:-3], refs[-3:]
    feats = grad_weight.shape[0]
    grad_weight[...] = (own[pl.ds(0, feats), :] + other[pl.ds(0, feats), :]) * scale
    grad_bias[...] = (own[pl.ds(feats, 1), :] + other[pl.ds(feats, 1), :]) * scale
    total = parts[0][...]
    for part in parts[1:]:
        total = total + part[...].astype(F32)
    grad_features[...] = (total * live_row[0:1, :]).astype(BF16)


def local(features, adj_tiles, tile_src, tile_dst, tile_count, cluster_size, weight, bias, grad_out):
    clusters = cluster_size.shape[0]
    slots, width = adj_tiles.shape[:2]
    nodes, half = features.shape
    feats, hidden = weight.shape
    levels = lax.axis_size("rows").bit_length() - 1
    columns = (levels + 1) * nodes
    bias = bias.reshape(1, hidden)
    own = features.T
    other = partner(own, "cols", 1)
    pack, live, live_row, own = kernel_call(
        functools.partial(prepare_kernel, clusters),
        (
            near_out((nodes + feats + 16, hidden), BF16),
            near_out((nodes, hidden), F32),
            near_out((8, nodes), F32),
            near_out((half, nodes), BF16),
        ),
        [HBM] * 5,
        (cluster_size, grad_out, weight, bias, own),
        scratch=[pltpu.SMEM((clusters,), jnp.int32), pltpu.VMEM((1, hidden), F32), pltpu.SemaphoreType.DMA((5,))],
    )
    used = kernel_call(count_kernel, near_out((8, hidden), jnp.int32), [SMEM], (tile_count,))
    hi, lo = kernel_call(
        functools.partial(build_kernel, levels, clusters),
        (near_out((nodes, columns), BF16), near_out((nodes, columns), BF16)),
        [HBM] * 3 + [VMEM],
        (adj_tiles, tile_src, tile_dst, used),
        scratch=[
            pltpu.VMEM((nodes, columns + width), F32),
            pltpu.VMEM((slots, width, width), BF16),
            pltpu.SMEM((slots,), jnp.int32),
            pltpu.SMEM((slots,), jnp.int32),
            pltpu.SMEM((8, hidden), jnp.int32),
            pltpu.SemaphoreType.DMA((-(-slots // TILE_GROUP),)),
            pltpu.SemaphoreType.DMA((3,)),
        ],
    )
    table = kernel_call(merge_kernel, near_out((nodes, feats), BF16), [VMEM, VMEM, VMEM], (own, other, live))
    tables = [table]
    for bit in range(levels):
        tables.append(partner(table, "rows", 1 << bit))
    other_pack = partner(pack, "cols", 1)
    sums, agg, grad_pre, hidden_near = kernel_call(
        functools.partial(main_kernel, levels),
        (
            near_out((feats + 16, hidden), BF16),
            near_out((nodes, feats), BF16),
            near_out((nodes, hidden), BF16),
            near_out((nodes, hidden), BF16),
        ),
        [VMEM] * (levels + 5),
        (hi, lo, pack, live, *tables),
    )
    hidden_out, stays, *parts = kernel_call(
        functools.partial(spread_kernel, levels),
        [jax.ShapeDtypeStruct((nodes, hidden), BF16), near_out((half, nodes), F32)]
        + [near_out((half, nodes), BF16)] * levels,
        [VMEM] * 8,
        (hi, lo, agg, grad_pre, hidden_near, pack, other_pack, live),
        out_specs=[HBM] + [VMEM] * (levels + 1),
        scratch=[pltpu.SemaphoreType.DMA],
    )
    received = []
    for bit in range(levels):
        received.append(partner(parts[bit], "rows", 1 << bit))
    turns = sum_turns(levels)
    moved = []
    for turn, masks in enumerate(turns):
        if turn:
            sums = add([sums, *moved], F32 if turn + 1 == len(turns) else BF16)
        moved = []
        for mask in masks:
            moved.append(partner(sums, "rows", mask))
    grad_scale = 1.0 / math.sqrt(nodes * lax.axis_size("rows"))
    grad_weight, grad_bias, grad_features = kernel_call(
        functools.partial(finish_kernel, grad_scale),
        (
            jax.ShapeDtypeStruct((feats, hidden), F32),
            jax.ShapeDtypeStruct((1, hidden), F32),
            jax.ShapeDtypeStruct((half, nodes), BF16),
        ),
        [VMEM] * (levels + 4),
        (sums, *moved, live_row, stays, *received),
    )
    return (hidden_out, grad_weight, grad_bias.reshape(hidden), grad_features.T)


def sum_turns(levels):
    bits = list(reversed(range(1, levels)))
    turns = []
    while len(bits) > 1:
        high, low = 1 << bits.pop(0), 1 << bits.pop(0)
        turns.append([low, high, low | high])
    turns += [[1 << bit] for bit in bits]
    return turns + [[1]]


def solution(mesh):
    return jax.shard_map(
        local,
        mesh=mesh,
        in_specs=(
            P("rows", "cols"),
            P("rows", None, None),
            P("rows"),
            P("rows"),
            P("rows"),
            P("rows"),
            P(None, "cols"),
            P("cols"),
            P("rows", "cols"),
        ),
        out_specs=(P("rows", "cols"), P(None, "cols"), P("cols"), P("rows", "cols")),
        check_vma=False,
    )
```
